256 devices in a mesh: gx: 4 (over y), gy: 4 (over x), gz: 16 (over z, core).
Axes of the slice: x: 4, y: 4, z: 8, core: 2. Of those that a mesh axis runs over, the one named last changes fastest.
Arguments:
- rhs: float32 [4, 4, 16, 64, 1536], P('gx', 'gy', 'gz'), may hold values from -20 to 20
- dual_block: bfloat16 [4, 4, 16, 1536, 1536], P('gx', 'gy', 'gz'), may hold values from -1 to 4, as said below
- schur_block: bfloat16 [4, 4, 16, 1536, 1536], P('gx', 'gy', 'gz'), may hold values from -1 to 2, as said below
- dual_scale: float32 [4, 4, 16, 1536], P('gx', 'gy', 'gz'), may hold values from 0.5 to 1.5
- dof_order: int32 [4, 4, 16, 1536], P('gx', 'gy', 'gz'), may hold values from 0 to 1535, each once within a row
- modes: float32 [4, 4, 16, 1536, 24], P('gx', 'gy', 'gz'), may hold values from -0.21875 to 0.21875
- coarse_inverse: float32 [6144, 6144], P(('gx', 'gy', 'gz')), may hold values from -1 to 4, as said below
- step_scale: float32 [2], replicated, may hold values from 0.5 to 1
Outputs:
- multipliers: float32 [4, 4, 16, 64, 1536], P('gx', 'gy', 'gz')
- residual: float32 [4, 4, 16, 64, 1536], P('gx', 'gy', 'gz')
The draws below stay inside these ranges and needn't reach their ends.
Inputs may be any that keep to these rules, and one draw needn't show every extreme that they name: For each subdomain, dof_order is a permutation of 0 to 1535. `dual_block`: Symmetric. `schur_block`: Symmetric. `coarse_inverse`: Symmetric.
All inputs are finite; a program needn't handle non-finite values.
Results may differ from the reference program's by a relative error of at most 0.0045.
Values sent between devices are 32-bit elements; how exact they have to be, the bound alone decides.
No kernel may reach another device: no remote copies, remote signals or barrier semaphores. Data moves between devices by JAX's collectives and lax.ppermute only.
A program may use at most 128 MiB of HBM per device.

```python
import jax
import jax.numpy as jnp
from jax import lax

FACE = 256
MODES = 24
LOADS = 64
ITERS = 2
M = 1536
NC = 6144
N_GX = 4
N_GY = 4
N_GZ = 16


def draw_rhs(key, part):
    count = N_GX * N_GY * N_GZ
    base = jax.random.normal(key, (N_GX, N_GY, N_GZ, LOADS, M), jnp.float32)
    base = jnp.clip(base, -6.0, 6.0)
    ramp = 1.0 + 2.0 * jnp.arange(count, dtype=jnp.float32) / max(count - 1, 1)
    ramp = ramp.reshape(N_GX, N_GY, N_GZ)
    return (base * ramp[:, :, :, None, None]).astype(jnp.float32)


def draw_block(key, lowest, highest, coupling):
    count = N_GX * N_GY * N_GZ
    keys = jax.random.split(key, count)

    def single(local_key):
        noise = jax.random.normal(local_key, (M, M), jnp.float32)
        offdiag = (noise + noise.T) * (coupling / (2.0 * jnp.sqrt(2.0 * M)))
        diagonal = jax.random.uniform(jax.random.fold_in(local_key, 1), (M,), jnp.float32, lowest, highest)
        return (offdiag + jnp.diag(diagonal)).astype(jnp.bfloat16)
    return lax.map(single, keys).reshape(N_GX, N_GY, N_GZ, M, M)


def draw_dual_block(key, part):
    return draw_block(jax.random.fold_in(key, 11), 1.5, 3.0, 0.8)


def draw_schur_block(key, part):
    return draw_block(jax.random.fold_in(key, 23), 0.5, 1.5, 0.4)


def draw_coarse_inverse(key, part):
    noise = jax.random.normal(key, (NC, NC), jnp.float32)
    offdiag = (noise + noise.T) / jnp.sqrt(2.0 * NC)
    diagonal = jax.random.uniform(jax.random.fold_in(key, 3), (NC,), jnp.float32, 1.0, 3.0)
    return (offdiag + jnp.diag(diagonal)).astype(jnp.float32)


def levels(stream_key, shape, cuts, smallest, largest):
    factor_of = 1.0
    for position, blocks in cuts:
        draws = jax.random.uniform(jax.random.fold_in(jax.random.fold_in(stream_key, 6), position), (blocks,), jnp.float32, smallest / len(cuts), largest / len(cuts))
        factor_of = factor_of * jnp.repeat(jnp.exp(draws), shape[position] // blocks).reshape((-1,) + (1,) * (len(shape) - 1 - position))
    return factor_of


def normal_values(rng, dims, scale, most, cuts=(), kind=jnp.bfloat16):
    values = jax.random.normal(rng, dims, jnp.float32) * scale
    if len(cuts) > 0:
        values = levels(rng, dims, cuts, -0.22, 0.18) * values
    return jnp.clip(values, min=-most, max=most).astype(kind)


def setup_inputs(seed: int = 0) -> dict:
    key_list = jax.random.split(jax.random.key(seed), 9)
    rhs = draw_rhs(jax.random.fold_in(key_list[8], 71), 0)
    dual_block = draw_dual_block(jax.random.fold_in(key_list[8], 71), 0)
    schur_block = draw_schur_block(jax.random.fold_in(key_list[8], 71), 0)
    dual_scale = jnp.clip(1.0 + 0.1 * jax.random.normal(key_list[3], (N_GX, N_GY, N_GZ, M), jnp.float32), 0.5, 1.5)
    dof_order = jax.vmap(lambda own: jax.random.permutation(own, M))(jax.random.split(key_list[4], N_GX * N_GY * N_GZ)).reshape((N_GX, N_GY, N_GZ, M)).astype(jnp.int32)
    modes = normal_values(key_list[5], (N_GX, N_GY, N_GZ, M, MODES), (M // 2) ** -0.5, 0.21875, ((0, 4), (1, 4), (2, 16)), jnp.float32)
    coarse_inverse = draw_coarse_inverse(jax.random.fold_in(key_list[8], 71), 0)
    step_scale = jnp.clip(jax.random.uniform(key_list[7], (ITERS,), jnp.float32, 0.5, 1.0), 0.5, 1.0)
    return dict(rhs=rhs, dual_block=dual_block, schur_block=schur_block, dual_scale=dual_scale, dof_order=dof_order, modes=modes, coarse_inverse=coarse_inverse, step_scale=step_scale)


HIGH = lax.Precision.HIGHEST


def shifted(field, axis, offset):
    length = field.shape[axis]
    zeros = jnp.zeros_like(lax.slice_in_dim(field, 0, 1, axis=axis))
    if offset > 0:
        return jnp.concatenate([zeros, lax.slice_in_dim(field, 0, length - 1, axis=axis)], axis)
    return jnp.concatenate([lax.slice_in_dim(field, 1, length, axis=axis), zeros], axis)


def assemble(field):
    faces = field.reshape(field.shape[:4] + (6, FACE))
    parts = []
    for direction in range(3):
        lower = faces[:, :, :, :, 2 * direction, :]
        upper = faces[:, :, :, :, 2 * direction + 1, :]
        parts.append(lower + shifted(upper, direction, 1))
        parts.append(upper + shifted(lower, direction, -1))
    return jnp.stack(parts, axis=4).reshape(field.shape)


def through(matrix, vector, order):
    count = N_GX * N_GY * N_GZ

    def single(items):
        block, values, places = items
        inverse = jnp.zeros((M,), jnp.int32).at[places].set(jnp.arange(M, dtype=jnp.int32))
        placed = jnp.take(values, inverse, axis=1).astype(jnp.float32)
        image = jnp.dot(placed, block.astype(jnp.float32), precision=HIGH)
        return jnp.take(image, places, axis=1)

    result = lax.map(single, (matrix.reshape(count, M, M), vector.reshape(count, LOADS, M), order.reshape(count, M)))
    return result.reshape(vector.shape)


def project(field, modes, coarse_inverse):
    count = N_GX * N_GY * N_GZ
    flat = field.reshape(count, LOADS, M)
    basis = modes.reshape(count, M, MODES)
    weights = jnp.einsum("dlm,dmk->ldk", flat, basis, precision=HIGH).reshape(LOADS, NC)
    solved = jnp.dot(weights, coarse_inverse, precision=HIGH).reshape(LOADS, count, MODES)
    correction = jnp.einsum("ldk,dmk->dlm", solved, basis, precision=HIGH).reshape(field.shape)
    return field - assemble(correction)


def reference(rhs, dual_block, schur_block, dual_scale, dof_order, modes, coarse_inverse, step_scale):
    scale = dual_scale[:, :, :, None, :]
    residual = rhs
    multipliers = jnp.zeros_like(rhs)
    for iteration in range(ITERS):
        search = project(assemble(through(schur_block, residual.astype(jnp.bfloat16), dof_order)), modes, coarse_inverse)
        image = scale * through(dual_block, (scale * search).astype(jnp.bfloat16), dof_order)
        image = project(assemble(image), modes, coarse_inverse)
        along = jnp.sum(residual * image, axis=(0, 1, 2, 4))
        energy = jnp.sum(image * image, axis=(0, 1, 2, 4))
        alpha = step_scale[iteration] * along / (energy + 1e-6)
        multipliers = multipliers + alpha[:, None] * search
        residual = residual - alpha[:, None] * image
    return multipliers, residual
```

```python
import jax
import jax.numpy as jnp
from jax import lax
from jax.experimental import pallas as pl
from jax.experimental.pallas import tpu as pltpu
from jax.sharding import Mesh
from jax.sharding import PartitionSpec as P

F32 = jnp.float32
BF16 = jnp.bfloat16

LOADS = 64
MODES = 24
FACE = 256
M = 6 * FACE
N_X, N_Y, N_Z = 4, 4, 16
PLANE = N_X * N_Y
CHIPS = N_Z // 2
COLS = N_Z * MODES
ROWS = PLANE * MODES
Z = ("gc", "core")
NT = (((1,), (1,)), ((), ()))
NN = (((1,), (0,)), ((), ()))

VMEM = pl.BlockSpec(memory_space=pltpu.VMEM)
SMEM = pl.BlockSpec(memory_space=pltpu.SMEM)


def mm(a, b, dims=NN):
    return lax.dot_general(a, b, dims, preferred_element_type=F32)


def split(value):
    high = value.astype(BF16)
    return high, (value - high.astype(F32)).astype(BF16)


def call(body, outs, args, scalars=1, scratch=(), name=None):
    return pl.pallas_call(
        body,
        out_shape=outs,
        in_specs=[SMEM] * scalars + [VMEM] * (len(args) - scalars),
        out_specs=jax.tree.map(lambda _: VMEM, outs),
        scratch_shapes=list(scratch),
        compiler_params=pltpu.CompilerParams(vmem_limit_bytes=40 * 1024 * 1024),
        name=name,
    )(*args)


def out(*dims, dtype=F32):
    return jax.ShapeDtypeStruct(dims, dtype)


def place_of():
    at = [lax.axis_index("gx"), lax.axis_index("gy"), lax.axis_index(Z)]
    ends = [N_X - 1, N_Y - 1, N_Z - 1]
    even = [1 - a % 2 for a in at]
    lower = [jnp.minimum(a, 1) for a in at]
    upper = [jnp.minimum(e - a, 1) for a, e in zip(at, ends)]
    return jnp.stack(even + lower + upper).astype(jnp.int32)


def pairs(count, which):
    forward = [(i, (i + 1) % count) for i in range(which, count, 2)]
    return forward + [(b, a) for a, b in forward]


def swap(arrays):
    found = []
    for direction, (axis, count) in enumerate((("gx", N_X), ("gy", N_Y), (Z, N_Z))):
        for which in range(2):
            found.append(lax.ppermute(arrays[2 * direction + which], axis, pairs(count, which)))
    return found


def local_product(u, block, picks):
    rows = u.shape[0]
    placed = mm(u, picks, NT).astype(BF16)
    image = mm(placed, block)
    if rows == 2 * LOADS:
        image = image[:LOADS] + image[LOADS:]
    high, low = split(image)
    back = mm(jnp.concatenate([high, low], axis=0), picks)
    return back[:LOADS] + back[LOADS:]


def send_faces(place, w, sends, extra=None):
    for direction in range(3):
        even = place[direction] == 1
        lo = 2 * direction * FACE
        for array, row in ((w, 0), (extra, LOADS)):
            if array is None:
                continue
            lower = array[:, lo : lo + FACE]
            upper = array[:, lo + FACE : lo + 2 * FACE]
            height = array.shape[0]
            sends[2 * direction][row : row + height, :] = jnp.where(even, upper, lower)
            sends[2 * direction + 1][row : row + height, :] = jnp.where(even, lower, upper)


def picks_body(order, picks):
    for block in range(6):
        rows = lax.broadcasted_iota(jnp.int32, (FACE, M), 0) + block * FACE
        picks[block * FACE : (block + 1) * FACE, :] = jnp.where(rows == order[0:1, :], 1.0, 0.0).astype(BF16)


def coarse_body(*refs):
    blocks, (high, low) = refs[:5], refs[5:]
    for index, block in enumerate(blocks):
        h, l = split(block[...].T)
        high[index * COLS : (index + 1) * COLS, :] = h
        low[index * COLS : (index + 1) * COLS, :] = l


def first_body(place, r, block, picks, modes_t, w, *sends):
    value = local_product(r[...].astype(BF16), block[...], picks[...])
    w[...] = value
    send_faces(place, value, sends, modes_t[...])


def modes_body(place, modes_t, *refs):
    found, (high, low), full = refs[:6], refs[6:8], refs[8]
    full[...] = jnp.zeros((2 * 128, M), F32)
    full[0:MODES, :] = modes_t[...]

    def put(row, direction, source, gate_lower, gate_upper):
        lo = 2 * direction * FACE
        value = found[source][LOADS : LOADS + MODES, :]
        full[row : row + MODES, lo : lo + FACE] = jnp.where(gate_lower, value, 0.0)
        full[row : row + MODES, lo + FACE : lo + 2 * FACE] = jnp.where(gate_upper, value, 0.0)

    def gates(direction, which):
        even = place[direction] == (1 - which)
        odd = place[direction] == which
        return (
            jnp.logical_and(odd, place[3 + direction] == 1),
            jnp.logical_and(even, place[6 + direction] == 1),
        )

    for which in range(2):
        for direction in range(2):
            lower, upper = gates(direction, which)
            put(128 + (2 * direction + which) * MODES, direction, 2 * direction + which, lower, upper)
    even = place[2] == 1
    lo = 4 * FACE
    from_lower = jnp.where(even, found[5][LOADS : LOADS + MODES, :], found[4][LOADS : LOADS + MODES, :])
    from_upper = jnp.where(even, found[4][LOADS : LOADS + MODES, :], found[5][LOADS : LOADS + MODES, :])
    full[MODES : 2 * MODES, lo : lo + FACE] = jnp.where(place[5] == 1, from_lower, 0.0)
    full[2 * MODES : 3 * MODES, lo + FACE : lo + 2 * FACE] = jnp.where(place[8] == 1, from_upper, 0.0)
    h, l = split(full[...])
    high[...] = h
    low[...] = l


def assemble_body(place, w, *refs):
    found, modes_t = refs[:6], refs[6]
    partial = refs[7] if len(refs) == 10 else None
    a, pay = refs[-2:]
    for direction in range(3):
        even = place[direction] == 1
        lo = 2 * direction * FACE
        first = found[2 * direction][0:LOADS, :]
        second = found[2 * direction + 1][0:LOADS, :]
        from_lower = jnp.where(even, second, first)
        from_upper = jnp.where(even, first, second)
        a[:, lo : lo + FACE] = w[:, lo : lo + FACE] + jnp.where(place[3 + direction] == 1, from_lower, 0.0)
        a[:, lo + FACE : lo + 2 * FACE] = w[:, lo + FACE : lo + 2 * FACE] + jnp.where(
            place[6 + direction] == 1, from_upper, 0.0
        )
    a_high, a_low = split(a[...])
    m = modes_t[...]
    m_high = m.astype(BF16).astype(F32)
    stack = jnp.concatenate([m_high, m - m_high], axis=0).astype(BF16)
    both = mm(stack, jnp.concatenate([a_high, a_low], axis=0), NT)
    both = both[:MODES] + both[MODES:]
    both = both + pltpu.roll(both, LOADS, 1)
    rest = jnp.zeros((8, 128), F32) if partial is None else partial[...]
    for p in range(PLANE):
        pay[p, 0:MODES, :] = both
        pay[p, MODES:32, :] = rest


def coarse_product_body(place, pay, high, low, keep, send, y):
    x = pay[:, 0:MODES, :].reshape(ROWS, 128)
    x_high, x_low = split(x)
    both = jnp.concatenate([x_high, x_low], axis=1)
    for block in range(5):
        rows = slice(block * COLS, (block + 1) * COLS)
        found = mm(high[rows, :], both)
        y[rows, :] = found[:, :128] + found[:, 128:] + mm(low[rows, :], x_high)
    rest = pay[0, MODES:32, :]
    for p in range(1, PLANE):
        rest = rest + pay[p, MODES:32, :]
    left = lax.broadcasted_iota(jnp.int32, (MODES, 128), 1) < LOADS
    even = place[2] == 1
    rest = jnp.concatenate([rest, jnp.zeros((MODES - 8, 128), F32)], axis=0)

    def at(block, z):
        row = block * COLS + (z % N_Z) * MODES
        return y[row : row + MODES, :]

    def chunk(z):
        return [
            jnp.where(left, at(0, z), at(1, z)),
            jnp.where(left, at(0, z - 1), at(2, z)),
            jnp.where(left, at(0, z + 1), at(3, z)),
            jnp.where(left, rest, at(4, z)),
        ]

    for c in range(CHIPS):
        for index, (zero, one) in enumerate(zip(chunk(2 * c), chunk(2 * c + 1))):
            rows = slice(index * MODES, (index + 1) * MODES)
            keep[c, rows, :] = jnp.where(even, zero, one)
            send[c, rows, :] = jnp.where(even, one, zero)


def corrected(a, q, m_high, m_low):
    y = q[0]
    for c in range(1, CHIPS):
        y = y + q[c]
    y_t = jnp.concatenate([y, jnp.zeros((32, 128), F32)], axis=0).T
    totals = y_t[:LOADS, 3 * MODES : 3 * MODES + 8]
    y_full = jnp.concatenate([y_t[:LOADS], y_t[LOADS:]], axis=1)
    y_high, y_low = split(y_full)
    found = mm(jnp.concatenate([y_high, y_low], axis=0), m_high[...])
    found = found[:LOADS] + found[LOADS:] + mm(y_high, m_low[...])
    return a[...] - found, totals


def products(first, second):
    lanes = lax.broadcasted_iota(jnp.int32, (LOADS, 128), 1)
    along = jnp.sum(first * second, axis=1, keepdims=True)
    energy = jnp.sum(second * second, axis=1, keepdims=True)
    both = jnp.where(lanes == 0, along, jnp.where(lanes == 1, energy, 0.0))
    return jnp.concatenate([both, both], axis=0).T[0:8, :]


def second_body(place, a, q, m_high, m_low, scale, block, picks, s, w, *sends):
    value, _ = corrected(a, q, m_high, m_low)
    s[...] = value
    found = scale[...] * local_product((scale[...] * value).astype(BF16), block[...], picks[...])
    w[...] = found
    send_faces(place, found, sends)


def third_body(place, a, q, m_high, m_low, r, block, picks, i, partial, w, *sends):
    value, _ = corrected(a, q, m_high, m_low)
    i[...] = value
    partial[...] = products(r[...], value)
    high, low = split(value)
    found = local_product(jnp.concatenate([high, low], axis=0), block[...], picks[...])
    w[...] = found
    send_faces(place, found, sends)


def fourth_body(place, steps, a, q, m_high, m_low, r, i, s, scale, block, picks, mult, s2, r1, w, *sends):
    t, totals = corrected(a, q, m_high, m_low)
    alpha = steps[0] * totals[:, 0:1] / (totals[:, 1:2] + 1e-6)
    value = s[...] - alpha * t
    s2[...] = value
    mult[...] = alpha * s[...]
    r1[...] = r[...] - alpha * i[...]
    found = scale[...] * local_product((scale[...] * value).astype(BF16), block[...], picks[...])
    w[...] = found
    send_faces(place, found, sends)


def fifth_body(a, q, m_high, m_low, r1, i, pay):
    value, _ = corrected(a, q, m_high, m_low)
    i[...] = value
    partial = products(r1[...], value)
    for p in range(PLANE):
        pay[p] = partial


def last_body(steps, q, mult, s2, r1, i, multipliers, residual):
    total = q[0]
    for c in range(1, CHIPS):
        total = total + q[c]
    columns = jnp.concatenate([total, jnp.zeros((120, 128), F32)], axis=0).T
    alpha = steps[1] * columns[:LOADS, 0:1] / (columns[:LOADS, 1:2] + 1e-6)
    multipliers[...] = mult[...] + alpha * s2[...]
    residual[...] = r1[...] - alpha * i[...]


def spread(array, axes):
    return lax.all_to_all(array, axes, 0, 0, tiled=True)


def other_core(array):
    return lax.ppermute(array, "core", [(0, 1), (1, 0)])


def shards(rhs, dual_block, schur_block, dual_scale, dof_order, modes, coarse_inverse, step_scale):
    place = place_of()
    r0 = rhs[0, 0, 0]
    dual = dual_block[0, 0, 0]
    schur = schur_block[0, 0, 0]
    scale = dual_scale[0, 0, 0]
    scale = scale.reshape(1, M)
    order = dof_order[0, 0, 0].reshape(1, M)
    modes_t = modes[0, 0, 0].T

    own = spread(coarse_inverse.reshape(MODES, PLANE, COLS).transpose(1, 0, 2), ("gx", "gy")).reshape(ROWS, COLS)
    near = [own]
    for axis, count in (("gx", N_X), ("gy", N_Y)):
        for which in range(2):
            near.append(lax.ppermute(own, axis, pairs(count, which)))

    picks = call(picks_body, out(M, M, dtype=BF16), (order,), 0, name="picks")
    field = out(LOADS, M)
    faces = [out(LOADS, FACE)] * 6

    w, *sends = call(
        first_body, [field] + [out(LOADS + MODES, FACE)] * 6, (place, r0, schur, picks, modes_t), name="first"
    )
    found = swap(sends)
    m_high, m_low = call(
        modes_body,
        [out(256, M, dtype=BF16)] * 2,
        (place, modes_t, *found),
        scratch=[pltpu.VMEM((256, M), F32)],
        name="modes",
    )
    c_high, c_low = call(coarse_body, [out(5 * COLS, ROWS, dtype=BF16)] * 2, near, 0, name="coarse")

    def project(w, found, partial=()):
        a, pay = call(
            assemble_body, [field, out(PLANE, 32, 128)], (place, w, *found, modes_t, *partial), name="assemble"
        )
        pay = spread(pay, ("gx", "gy"))
        keep, send = call(
            coarse_product_body,
            [out(CHIPS, 96, 128)] * 2,
            (place, pay, c_high, c_low),
            scratch=[pltpu.VMEM((5 * COLS, 128), F32)],
            name="product",
        )
        return a, spread(keep + other_core(send), "gc")

    a, q = project(w, found)
    s, w, *sends = call(
        second_body, [field, field] + faces, (place, a, q, m_high, m_low, scale, dual, picks), name="second"
    )
    a, q = project(w, swap(sends))
    i, partial, w, *sends = call(
        third_body,
        [field, out(8, 128), field] + faces,
        (place, a, q, m_high, m_low, r0, schur, picks),
        name="third",
    )
    a, q = project(w, swap(sends), (partial,))
    mult, s2, r1, w, *sends = call(
        fourth_body,
        [field] * 4 + faces,
        (place, step_scale, a, q, m_high, m_low, r0, i, s, scale, dual, picks),
        2,
        name="fourth",
    )
    a, q = project(w, swap(sends))
    i2, pay = call(fifth_body, [field, out(PLANE, 8, 128)], (a, q, m_high, m_low, r1), 0, name="fifth")
    total = jnp.sum(spread(pay, ("gx", "gy")), axis=0)
    total = total + other_core(total)
    q = spread(jnp.broadcast_to(total, (CHIPS, 8, 128)), "gc")
    multipliers, residual = call(last_body, [field] * 2, (step_scale, q, mult, s2, r1, i2), name="last")
    return (multipliers[None, None, None], residual[None, None, None])


def solution(mesh):
    mesh = Mesh(mesh.devices.reshape(N_X, N_Y, CHIPS, 2), ("gx", "gy", "gc", "core"))
    cell = lambda rest: P("gx", "gy", Z, *([None] * rest))
    in_specs = (cell(2), cell(2), cell(2), cell(1), cell(1), cell(2), P(("gx", "gy", "gc", "core"), None), P())
    return jax.shard_map(shards, mesh=mesh, in_specs=in_specs, out_specs=(cell(2), cell(2)), check_vma=False)
```

```python
import jax
import jax.numpy as jnp
from jax import lax
from jax.experimental import pallas as pl
from jax.experimental.pallas import tpu as pltpu
from jax.sharding import Mesh
from jax.sharding import PartitionSpec as P

F32 = jnp.float32
BF16 = jnp.bfloat16

LOADS = 64
MODES = 24
FACE = 256
M = 6 * FACE
N_X, N_Y, N_Z = 4, 4, 16
PLANE = N_X * N_Y
CHIPS = N_Z // 2
COLS = N_Z * MODES
ROWS = PLANE * MODES
Z = ("gc", "core")
NT = (((1,), (1,)), ((), ()))
NN = (((1,), (0,)), ((), ()))

VMEM = pl.BlockSpec(memory_space=pltpu.VMEM)
SMEM = pl.BlockSpec(memory_space=pltpu.SMEM)


def mm(a, b, dims=NN):
    return lax.dot_general(a, b, dims, preferred_element_type=F32)


def split(value):
    high = value.astype(BF16)
    return high, (value - high.astype(F32)).astype(BF16)


def call(body, outs, args, scalars=1, scratch=(), name=None):
    return pl.pallas_call(
        body,
        out_shape=outs,
        in_specs=[SMEM] * scalars + [VMEM] * (len(args) - scalars),
        out_specs=jax.tree.map(lambda _: VMEM, outs),
        scratch_shapes=list(scratch),
        compiler_params=pltpu.CompilerParams(vmem_limit_bytes=16 * 1024 * 1024),
        name=name,
    )(*args)


def out(*dims, dtype=F32):
    return jax.ShapeDtypeStruct(dims, dtype)


def place_body(place):
    at = [lax.axis_index("gx"), lax.axis_index("gy"), 2 * lax.axis_index("gc") + lax.axis_index("core")]
    for direction, (index, end) in enumerate(zip(at, (N_X - 1, N_Y - 1, N_Z - 1))):
        place[direction] = 1 - index % 2
        place[3 + direction] = jnp.minimum(index, 1)
        place[6 + direction] = jnp.minimum(end - index, 1)


def pairs(count, which):
    forward = [(i, (i + 1) % count) for i in range(which, count, 2)]
    return forward + [(b, a) for a, b in forward]


def swap(arrays):
    found = []
    for direction, (axis, count) in enumerate((("gx", N_X), ("gy", N_Y), (Z, N_Z))):
        for which in range(2):
            found.append(lax.ppermute(arrays[2 * direction + which], axis, pairs(count, which)))
    return found


def local_product(u, block, picks):
    rows = u.shape[0]
    placed = mm(u, picks, NT).astype(BF16)
    image = mm(placed, block)
    if rows == 2 * LOADS:
        image = image[:LOADS] + image[LOADS:]
    high, low = split(image)
    back = mm(jnp.concatenate([high, low], axis=0), picks)
    return back[:LOADS] + back[LOADS:]


def send_faces(place, w, sends, extra=None):
    for direction in range(3):
        even = place[direction] == 1
        lo = 2 * direction * FACE
        for array, row in ((w, 0), (extra, LOADS)):
            if array is None:
                continue
            lower = array[:, lo : lo + FACE]
            upper = array[:, lo + FACE : lo + 2 * FACE]
            height = array.shape[0]
            sends[2 * direction][row : row + height, :] = jnp.where(even, upper, lower)
            sends[2 * direction + 1][row : row + height, :] = jnp.where(even, lower, upper)


def picks_body(order, picks):
    for block in range(6):
        rows = lax.broadcasted_iota(jnp.int32, (FACE, M), 0) + block * FACE
        picks[block * FACE : (block + 1) * FACE, :] = jnp.where(rows == order[0:1, :], 1.0, 0.0).astype(BF16)


def coarse_body(*refs):
    blocks, (high, low) = refs[:5], refs[5:]
    for index, block in enumerate(blocks):
        parts = block[...].reshape(PLANE, MODES, COLS)
        ordered = [parts[:, :16].reshape(PLANE * 16, COLS), parts[:, 16:].reshape(PLANE * 8, COLS)]
        h, l = split(jnp.concatenate(ordered, axis=0).T)
        high[index * COLS : (index + 1) * COLS, :] = h
        low[index * COLS : (index + 1) * COLS, :] = l


def first_body(place, r, block, picks, modes_t, w, *sends):
    value = local_product(r[...].astype(BF16), block[...], picks[...])
    w[...] = value
    send_faces(place, value, sends, modes_t[...])


def modes_body(place, modes_t, *refs):
    found, (high, low), full = refs[:6], refs[6:8], refs[8]
    full[...] = jnp.zeros((2 * 128, M), F32)
    full[0:MODES, :] = modes_t[...]

    def put(row, direction, source, gate_lower, gate_upper):
        lo = 2 * direction * FACE
        value = found[source][LOADS : LOADS + MODES, :]
        full[row : row + MODES, lo : lo + FACE] = jnp.where(gate_lower, value, 0.0)
        full[row : row + MODES, lo + FACE : lo + 2 * FACE] = jnp.where(gate_upper, value, 0.0)

    def gates(direction, which):
        even = place[direction] == (1 - which)
        odd = place[direction] == which
        return (
            jnp.logical_and(odd, place[3 + direction] == 1),
            jnp.logical_and(even, place[6 + direction] == 1),
        )

    for which in range(2):
        for direction in range(2):
            lower, upper = gates(direction, which)
            put(128 + (2 * direction + which) * MODES, direction, 2 * direction + which, lower, upper)
    even = place[2] == 1
    lo = 4 * FACE
    from_lower = jnp.where(even, found[5][LOADS : LOADS + MODES, :], found[4][LOADS : LOADS + MODES, :])
    from_upper = jnp.where(even, found[4][LOADS : LOADS + MODES, :], found[5][LOADS : LOADS + MODES, :])
    full[MODES : 2 * MODES, lo : lo + FACE] = jnp.where(place[5] == 1, from_lower, 0.0)
    full[2 * MODES : 3 * MODES, lo + FACE : lo + 2 * FACE] = jnp.where(place[8] == 1, from_upper, 0.0)
    h, l = split(full[...])
    high[...] = h
    low[...] = l


def assemble_body(place, w, *refs):
    found, modes_t = refs[:6], refs[6]
    partial = refs[7] if len(refs) == 10 else None
    a, pay = refs[-2:]
    for direction in range(3):
        even = place[direction] == 1
        lo = 2 * direction * FACE
        first = found[2 * direction][0:LOADS, :]
        second = found[2 * direction + 1][0:LOADS, :]
        from_lower = jnp.where(even, second, first)
        from_upper = jnp.where(even, first, second)
        a[:, lo : lo + FACE] = w[:, lo : lo + FACE] + jnp.where(place[3 + direction] == 1, from_lower, 0.0)
        a[:, lo + FACE : lo + 2 * FACE] = w[:, lo + FACE : lo + 2 * FACE] + jnp.where(
            place[6 + direction] == 1, from_upper, 0.0
        )
    a_high, a_low = split(a[...])
    m = modes_t[...]
    m_high = m.astype(BF16).astype(F32)
    stack = jnp.concatenate([m_high, m - m_high], axis=0).astype(BF16)
    both = mm(stack, jnp.concatenate([a_high, a_low], axis=0), NT)
    both = both[:MODES] + both[MODES:]
    both = both + pltpu.roll(both, LOADS, 1)
    rest = jnp.zeros((8, 128), F32) if partial is None else partial[...]
    left = lax.broadcasted_iota(jnp.int32, (16, 128), 1) < LOADS
    packed = jnp.where(left, both[:16], jnp.concatenate([both[16:], rest], axis=0))
    for p in range(PLANE):
        pay[p] = packed


def coarse_product_body(place, pay, high, low, keep, send, y):
    def half(rows, keep_left):
        value = pay[:, 0:rows, :].reshape(PLANE * rows, 128)
        left = lax.broadcasted_iota(jnp.int32, value.shape, 1) < LOADS
        return jnp.where(left == keep_left, value, pltpu.roll(value, LOADS, 1))

    x_high, x_low = split(jnp.concatenate([half(16, True), half(8, False)], axis=0))
    both = jnp.concatenate([x_high, x_low], axis=1)
    for block in range(5):
        rows = slice(block * COLS, (block + 1) * COLS)
        found = mm(high[rows, :], both)
        y[rows, :] = found[:, :128] + found[:, 128:] + mm(low[rows, :], x_high)
    rest = pay[0, 8:16, :]
    for p in range(1, PLANE):
        rest = rest + pay[p, 8:16, :]
    rest = pltpu.roll(rest, LOADS, 1)
    left = lax.broadcasted_iota(jnp.int32, (MODES, 128), 1) < LOADS
    even = place[2] == 1
    rest = jnp.concatenate([rest, jnp.zeros((MODES - 8, 128), F32)], axis=0)

    def at(block, z):
        row = block * COLS + (z % N_Z) * MODES
        return y[row : row + MODES, :]

    def chunk(z):
        return [
            jnp.where(left, at(0, z), at(1, z)),
            jnp.where(left, at(0, z - 1), at(2, z)),
            jnp.where(left, at(0, z + 1), at(3, z)),
            jnp.where(left, rest, at(4, z)),
        ]

    for c in range(CHIPS):
        for index, (zero, one) in enumerate(zip(chunk(2 * c), chunk(2 * c + 1))):
            rows = slice(index * MODES, (index + 1) * MODES)
            keep[c, rows, :] = jnp.where(even, zero, one)
            send[c, rows, :] = jnp.where(even, one, zero)


def corrected(a, q, m_high, m_low):
    y = q[0]
    for c in range(1, CHIPS):
        y = y + q[c]
    y_t = jnp.concatenate([y, jnp.zeros((32, 128), F32)], axis=0).T
    totals = y_t[:LOADS, 3 * MODES : 3 * MODES + 8]
    y_full = jnp.concatenate([y_t[:LOADS], y_t[LOADS:]], axis=1)
    y_high, y_low = split(y_full)
    found = mm(jnp.concatenate([y_high, y_low], axis=0), m_high[...])
    found = found[:LOADS] + found[LOADS:] + mm(y_high, m_low[...])
    return a[...] - found, totals


def products(first, second):
    lanes = lax.broadcasted_iota(jnp.int32, (LOADS, 128), 1)
    along = jnp.sum(first * second, axis=1, keepdims=True)
    energy = jnp.sum(second * second, axis=1, keepdims=True)
    both = jnp.where(lanes == 0, along, jnp.where(lanes == 1, energy, 0.0))
    return jnp.concatenate([both, both], axis=0).T[0:8, :]


def second_body(place, a, q, m_high, m_low, scale, block, picks, s, w, *sends):
    value, _ = corrected(a, q, m_high, m_low)
    s[...] = value
    found = scale[...] * local_product((scale[...] * value).astype(BF16), block[...], picks[...])
    w[...] = found
    send_faces(place, found, sends)


def third_body(place, a, q, m_high, m_low, r, block, picks, i, partial, w, *sends):
    value, _ = corrected(a, q, m_high, m_low)
    i[...] = value
    partial[...] = products(r[...], value)
    high, low = split(value)
    found = local_product(jnp.concatenate([high, low], axis=0), block[...], picks[...])
    w[...] = found
    send_faces(place, found, sends)


def fourth_body(place, steps, a, q, m_high, m_low, r, i, s, scale, block, picks, mult, s2, r1, w, *sends):
    t, totals = corrected(a, q, m_high, m_low)
    alpha = steps[0] * totals[:, 0:1] / (totals[:, 1:2] + 1e-6)
    value = s[...] - alpha * t
    s2[...] = value
    mult[...] = alpha * s[...]
    r1[...] = r[...] - alpha * i[...]
    found = scale[...] * local_product((scale[...] * value).astype(BF16), block[...], picks[...])
    w[...] = found
    send_faces(place, found, sends)


def fifth_body(a, q, m_high, m_low, r1, i, pay):
    value, _ = corrected(a, q, m_high, m_low)
    i[...] = value
    partial = products(r1[...], value)
    for p in range(PLANE):
        pay[p] = partial


def sum_body(pay, total):
    value = pay[0]
    for p in range(1, PLANE):
        value = value + pay[p]
    total[...] = value


def share_body(mine, other, copies):
    for c in range(CHIPS):
        copies[c] = mine[...] + other[...]


def last_body(steps, q, mult, s2, r1, i, multipliers, residual):
    total = q[0]
    for c in range(1, CHIPS):
        total = total + q[c]
    columns = jnp.concatenate([total, jnp.zeros((120, 128), F32)], axis=0).T
    alpha = steps[1] * columns[:LOADS, 0:1] / (columns[:LOADS, 1:2] + 1e-6)
    multipliers[...] = mult[...] + alpha * s2[...]
    residual[...] = r1[...] - alpha * i[...]


def spread(array, axes):
    return lax.all_to_all(array, axes, 0, 0, tiled=True)


def other_core(array):
    return lax.ppermute(array, "core", [(0, 1), (1, 0)])


def shards(rhs, dual_block, schur_block, dual_scale, dof_order, modes, coarse_inverse, step_scale):
    place = pl.pallas_call(place_body, out_shape=out(9, dtype=jnp.int32), out_specs=SMEM, name="place")()
    r0 = rhs[0, 0, 0]
    dual = dual_block[0, 0, 0]
    schur = schur_block[0, 0, 0]
    scale = dual_scale[0, 0, 0]
    scale = scale.reshape(1, M)
    order = dof_order[0, 0, 0].reshape(1, M)
    modes_t = modes[0, 0, 0].T

    own = spread(coarse_inverse.reshape(MODES, PLANE, COLS).transpose(1, 0, 2), ("gx", "gy")).reshape(ROWS, COLS)
    near = [own]
    for axis, count in (("gx", N_X), ("gy", N_Y)):
        for which in range(2):
            near.append(lax.ppermute(own, axis, pairs(count, which)))

    picks = call(picks_body, out(M, M, dtype=BF16), (order,), 0, name="picks")
    field = out(LOADS, M)
    faces = [out(LOADS, FACE)] * 6

    w, *sends = call(
        first_body, [field] + [out(LOADS + MODES, FACE)] * 6, (place, r0, schur, picks, modes_t), name="first"
    )
    found = swap(sends)
    m_high, m_low = call(
        modes_body,
        [out(256, M, dtype=BF16)] * 2,
        (place, modes_t, *found),
        scratch=[pltpu.VMEM((256, M), F32)],
        name="modes",
    )
    c_high, c_low = call(coarse_body, [out(5 * COLS, ROWS, dtype=BF16)] * 2, near, 0, name="coarse")

    def weigh(w, found, partial=()):
        return call(
            assemble_body, [field, out(PLANE, 16, 128)], (place, w, *found, modes_t, *partial), name="assemble"
        )

    def solve(pay):
        pay = spread(pay, ("gx", "gy"))
        keep, send = call(
            coarse_product_body,
            [out(CHIPS, 96, 128)] * 2,
            (place, pay, c_high, c_low),
            scratch=[pltpu.VMEM((5 * COLS, 128), F32)],
            name="product",
        )
        return spread(keep + other_core(send), "gc")

    def project(w, found, partial=()):
        a, pay = weigh(w, found, partial)
        return a, solve(pay)

    a, pay = weigh(w, found)
    pay, c_high, c_low, m_high, m_low = lax.optimization_barrier((pay, c_high, c_low, m_high, m_low))
    q = solve(pay)
    s, w, *sends = call(
        second_body, [field, field] + faces, (place, a, q, m_high, m_low, scale, dual, picks), name="second"
    )
    a, q = project(w, swap(sends))
    i, partial, w, *sends = call(
        third_body,
        [field, out(8, 128), field] + faces,
        (place, a, q, m_high, m_low, r0, schur, picks),
        name="third",
    )
    a, q = project(w, swap(sends), (partial,))
    mult, s2, r1, w, *sends = call(
        fourth_body,
        [field] * 4 + faces,
        (place, step_scale, a, q, m_high, m_low, r0, i, s, scale, dual, picks),
        2,
        name="fourth",
    )
    a, q = project(w, swap(sends))
    i2, pay = call(fifth_body, [field, out(PLANE, 8, 128)], (a, q, m_high, m_low, r1), 0, name="fifth")
    total = call(sum_body, out(8, 128), (spread(pay, ("gx", "gy")),), 0, name="sum")
    q = spread(call(share_body, out(CHIPS, 8, 128), (total, other_core(total)), 0, name="share"), "gc")
    multipliers, residual = call(last_body, [field] * 2, (step_scale, q, mult, s2, r1, i2), name="last")
    return (multipliers[None, None, None], residual[None, None, None])


def solution(mesh):
    mesh = Mesh(mesh.devices.reshape(N_X, N_Y, CHIPS, 2), ("gx", "gy", "gc", "core"))
    cell = lambda rest: P("gx", "gy", Z, *([None] * rest))
    in_specs = (cell(2), cell(2), cell(2), cell(1), cell(1), cell(2), P(("gx", "gy", "gc", "core"), None), P())
    return jax.shard_map(shards, mesh=mesh, in_specs=in_specs, out_specs=(cell(2), cell(2)), check_vma=False)
```

```python
import jax
import jax.numpy as jnp
from jax import lax
from jax.experimental import pallas as pl
from jax.experimental.pallas import tpu as pltpu
from jax.sharding import Mesh
from jax.sharding import PartitionSpec as P

F32 = jnp.float32
BF16 = jnp.bfloat16

LOADS = 64
MODES = 24
FACE = 256
M = 6 * FACE
N_X, N_Y, N_Z = 4, 4, 16
PLANE = N_X * N_Y
CHIPS = N_Z // 2
LINE = N_Y * CHIPS
ROWS = LINE * MODES
COLS = N_X * 2 * MODES
SLOTS = 88
Z = ("gc", "core")
NT = (((1,), (1,)), ((), ()))
NN = (((1,), (0,)), ((), ()))

VMEM = pl.BlockSpec(memory_space=pltpu.VMEM)
SMEM = pl.BlockSpec(memory_space=pltpu.SMEM)


def mm(a, b, dims=NN):
    return lax.dot_general(a, b, dims, preferred_element_type=F32)


def split(value):
    high = value.astype(BF16)
    return high, (value - high.astype(F32)).astype(BF16)


def call(body, outs, args, scalars=1, scratch=(), name=None):
    return pl.pallas_call(
        body,
        out_shape=outs,
        in_specs=[SMEM] * scalars + [VMEM] * (len(args) - scalars),
        out_specs=jax.tree.map(lambda _: VMEM, outs),
        scratch_shapes=list(scratch),
        compiler_params=pltpu.CompilerParams(vmem_limit_bytes=16 * 1024 * 1024),
        name=name,
    )(*args)


def out(*dims, dtype=F32):
    return jax.ShapeDtypeStruct(dims, dtype)


def place_body(place):
    at = [lax.axis_index("gx"), lax.axis_index("gy"), 2 * lax.axis_index("gc") + lax.axis_index("core")]
    place[9] = 1 - lax.axis_index("gc") % 2
    for direction, (index, end) in enumerate(zip(at, (N_X - 1, N_Y - 1, N_Z - 1))):
        place[direction] = 1 - index % 2
        place[3 + direction] = jnp.minimum(index, 1)
        place[6 + direction] = jnp.minimum(end - index, 1)


def pairs(count, which):
    forward = [(i, (i + 1) % count) for i in range(which, count, 2)]
    return forward + [(b, a) for a, b in forward]


def swap(arrays):
    found = []
    for direction, (axis, count) in enumerate((("gx", N_X), ("gy", N_Y), (Z, N_Z))):
        for which in range(2):
            found.append(lax.ppermute(arrays[2 * direction + which], axis, pairs(count, which)))
    return found


def local_product(u, block, picks):
    rows = u.shape[0]
    placed = mm(u, picks, NT).astype(BF16)
    image = mm(placed, block)
    if rows == 2 * LOADS:
        image = image[:LOADS] + image[LOADS:]
    high, low = split(image)
    back = mm(jnp.concatenate([high, low], axis=0), picks)
    return back[:LOADS] + back[LOADS:]


def send_faces(place, w, sends, extra=None):
    for direction in range(3):
        even = place[direction] == 1
        lo = 2 * direction * FACE
        for array, row in ((w, 0), (extra, LOADS)):
            if array is None:
                continue
            lower = array[:, lo : lo + FACE]
            upper = array[:, lo + FACE : lo + 2 * FACE]
            height = array.shape[0]
            sends[2 * direction][row : row + height, :] = jnp.where(even, upper, lower)
            sends[2 * direction + 1][row : row + height, :] = jnp.where(even, lower, upper)


def picks_body(order, picks):
    for block in range(6):
        rows = lax.broadcasted_iota(jnp.int32, (FACE, M), 0) + block * FACE
        picks[block * FACE : (block + 1) * FACE, :] = jnp.where(rows == order[0:1, :], 1.0, 0.0).astype(BF16)


def deal_body(rows, dealt):
    for y in range(N_Y):
        for c in range(CHIPS):
            at = [x * (N_Y * N_Z * MODES) + (y * N_Z + 2 * c) * MODES for x in range(N_X)]
            chunk = jnp.concatenate([rows[:, a : a + 2 * MODES] for a in at], axis=1)
            rest = chunk[:, 128:]
            right = jnp.concatenate([rest[16:], jnp.zeros((8, 64), F32)], axis=0)
            dealt[y * CHIPS + c, 0:MODES, :] = chunk[:, :128]
            dealt[y * CHIPS + c, MODES:40, :] = jnp.concatenate([rest[:16], right], axis=1)


def coarse_body(*refs):
    blocks, (high, low) = refs[:5], refs[5:]
    for index, block in enumerate(blocks):

        def rows(first, last):
            return block[:, first:last, :].reshape(LINE * (last - first), 128)

        most = jnp.concatenate([rows(0, 16), rows(16, 24)], axis=0).T
        rest = jnp.concatenate([rows(24, 40), pltpu.roll(rows(24, 32), 64, 1)], axis=0).T
        h, l = split(jnp.concatenate([most, rest[:64]], axis=0))
        high[index * COLS : (index + 1) * COLS, :] = h
        low[index * COLS : (index + 1) * COLS, :] = l


def first_body(place, r, block, picks, modes_t, w, *sends):
    value = local_product(r[...].astype(BF16), block[...], picks[...])
    w[...] = value
    send_faces(place, value, sends, modes_t[...])


def modes_body(place, modes_t, *refs):
    found, (high, low), full = refs[:6], refs[6:8], refs[8]
    full[...] = jnp.zeros((2 * 128, M), F32)
    full[0:MODES, :] = modes_t[...]

    def put(rows, direction, source, gate_lower, gate_upper):
        lo = 2 * direction * FACE
        for row, first, last in rows:
            value = found[source][LOADS + first : LOADS + last, :]
            full[row : row + last - first, lo : lo + FACE] = jnp.where(gate_lower, value, 0.0)
            full[row : row + last - first, lo + FACE : lo + 2 * FACE] = jnp.where(gate_upper, value, 0.0)

    def gates(direction, which):
        even = place[direction] == (1 - which)
        odd = place[direction] == which
        return (
            jnp.logical_and(odd, place[3 + direction] == 1),
            jnp.logical_and(even, place[6 + direction] == 1),
        )

    for which in range(2):
        for direction in range(2):
            lower, upper = gates(direction, which)
            slot = 2 * direction + which
            rows = [(128 + slot * MODES, 0, MODES)] if slot < 3 else [(128 + 3 * MODES, 0, 16), (80, 16, MODES)]
            put(rows, direction, slot, lower, upper)
    even = place[2] == 1
    lo = 4 * FACE
    from_lower = jnp.where(even, found[5][LOADS : LOADS + MODES, :], found[4][LOADS : LOADS + MODES, :])
    from_upper = jnp.where(even, found[4][LOADS : LOADS + MODES, :], found[5][LOADS : LOADS + MODES, :])
    full[MODES : 2 * MODES, lo : lo + FACE] = jnp.where(place[5] == 1, from_lower, 0.0)
    full[2 * MODES : 3 * MODES, lo + FACE : lo + 2 * FACE] = jnp.where(place[8] == 1, from_upper, 0.0)
    h, l = split(full[...])
    high[...] = h
    low[...] = l


def assemble_body(place, w, *refs):
    found, modes_t = refs[:6], refs[6]
    partial = refs[7] if len(refs) == 10 else None
    a, pay = refs[-2:]
    for direction in range(3):
        even = place[direction] == 1
        lo = 2 * direction * FACE
        first = found[2 * direction][0:LOADS, :]
        second = found[2 * direction + 1][0:LOADS, :]
        from_lower = jnp.where(even, second, first)
        from_upper = jnp.where(even, first, second)
        a[:, lo : lo + FACE] = w[:, lo : lo + FACE] + jnp.where(place[3 + direction] == 1, from_lower, 0.0)
        a[:, lo + FACE : lo + 2 * FACE] = w[:, lo + FACE : lo + 2 * FACE] + jnp.where(
            place[6 + direction] == 1, from_upper, 0.0
        )
    a_high, a_low = split(a[...])
    m = modes_t[...]
    m_high = m.astype(BF16).astype(F32)
    stack = jnp.concatenate([m_high, m - m_high], axis=0).astype(BF16)
    both = mm(stack, jnp.concatenate([a_high, a_low], axis=0), NT)
    both = both[:MODES] + both[MODES:]
    both = both + pltpu.roll(both, LOADS, 1)
    rest = jnp.zeros((8, 128), F32) if partial is None else partial[...]
    left = lax.broadcasted_iota(jnp.int32, (16, 128), 1) < LOADS
    packed = jnp.where(left, both[:16], jnp.concatenate([both[16:], rest], axis=0))
    for p in range(LINE):
        pay[p] = packed


def coarse_product_body(place, pay, high, low, keep, send, y):
    def half(rows, keep_left):
        value = pay[:, 0:rows, :].reshape(LINE * rows, 128)
        left = lax.broadcasted_iota(jnp.int32, value.shape, 1) < LOADS
        return jnp.where(left == keep_left, value, pltpu.roll(value, LOADS, 1))

    x_high, x_low = split(jnp.concatenate([half(16, True), half(8, False)], axis=0))
    both = jnp.concatenate([x_high, x_low], axis=1)
    for block in range(5):
        rows = slice(block * COLS, (block + 1) * COLS)
        found = mm(high[rows, :], both)
        y[rows, :] = found[:, :128] + found[:, 128:] + mm(low[rows, :], x_high)
    rest = pay[0, 8:16, :]
    for p in range(1, LINE):
        rest = rest + pay[p, 8:16, :]
    rest = pltpu.roll(rest, LOADS, 1)
    left = lax.broadcasted_iota(jnp.int32, (MODES, 128), 1) < LOADS
    even = place[2] == 1
    even_chip = place[9] == 1

    def at(block, x, k):
        row = block * COLS + (x % N_X * 2 + k) * MODES
        return y[row : row + MODES, :]

    def chunk(x, k):
        before, after = (3, 4) if k == 0 else (4, 3)
        beyond = jnp.where(even_chip, at(after, x, 1 - k), at(before, x, 1 - k))
        beside = at(0, x, 1 - k)
        below, above = (beyond, beside) if k == 0 else (beside, beyond)
        last = at(2, x, k)
        tail = jnp.concatenate([rest, last[16:]], axis=0)
        return [
            jnp.where(left, at(0, x, k), at(0, x ^ 1, k)),
            jnp.where(left, below, at(0, x - 1 + 2 * (x % 2), k)),
            jnp.where(left, above, at(1, x, k)),
            jnp.where(left[:16], tail, last[:16]),
        ]

    for x in range(N_X):
        for index, (zero, one) in enumerate(zip(chunk(x, 0), chunk(x, 1))):
            rows = slice(index * MODES, index * MODES + zero.shape[0])
            keep[x, rows, :] = jnp.where(even, zero, one)
            send[x, rows, :] = jnp.where(even, one, zero)


def corrected(a, q, m_high, m_low):
    y = q[0]
    for x in range(1, N_X):
        y = y + q[x]
    y_t = jnp.concatenate([y, jnp.zeros((128 - SLOTS, 128), F32)], axis=0).T
    totals = y_t[:LOADS, 3 * MODES : 3 * MODES + 8]
    y_full = jnp.concatenate([y_t[:LOADS], y_t[LOADS:]], axis=1)
    y_high, y_low = split(y_full)
    found = mm(jnp.concatenate([y_high, y_low], axis=0), m_high[...])
    found = found[:LOADS] + found[LOADS:] + mm(y_high, m_low[...])
    return a[...] - found, totals


def products(first, second):
    lanes = lax.broadcasted_iota(jnp.int32, (LOADS, 128), 1)
    along = jnp.sum(first * second, axis=1, keepdims=True)
    energy = jnp.sum(second * second, axis=1, keepdims=True)
    both = jnp.where(lanes == 0, along, jnp.where(lanes == 1, energy, 0.0))
    return jnp.concatenate([both, both], axis=0).T[0:8, :]


def second_body(place, a, q, m_high, m_low, scale, block, picks, s, w, *sends):
    value, _ = corrected(a, q, m_high, m_low)
    s[...] = value
    found = scale[...] * local_product((scale[...] * value).astype(BF16), block[...], picks[...])
    w[...] = found
    send_faces(place, found, sends)


def third_body(place, a, q, m_high, m_low, r, block, picks, i, partial, w, *sends):
    value, _ = corrected(a, q, m_high, m_low)
    i[...] = value
    partial[...] = products(r[...], value)
    high, low = split(value)
    found = local_product(jnp.concatenate([high, low], axis=0), block[...], picks[...])
    w[...] = found
    send_faces(place, found, sends)


def fourth_body(place, steps, a, q, m_high, m_low, r, i, s, scale, block, picks, mult, s2, r1, w, *sends):
    t, totals = corrected(a, q, m_high, m_low)
    alpha = steps[0] * totals[:, 0:1] / (totals[:, 1:2] + 1e-6)
    value = s[...] - alpha * t
    s2[...] = value
    mult[...] = alpha * s[...]
    r1[...] = r[...] - alpha * i[...]
    found = scale[...] * local_product((scale[...] * value).astype(BF16), block[...], picks[...])
    w[...] = found
    send_faces(place, found, sends)


def fifth_body(a, q, m_high, m_low, r1, i, pay):
    value, _ = corrected(a, q, m_high, m_low)
    i[...] = value
    partial = products(r1[...], value)
    for p in range(PLANE):
        pay[p] = partial


def sum_body(pay, total):
    value = pay[0]
    for p in range(1, PLANE):
        value = value + pay[p]
    total[...] = value


def share_body(mine, other, copies):
    for c in range(CHIPS):
        copies[c] = mine[...] + other[...]


def last_body(steps, q, mult, s2, r1, i, multipliers, residual):
    total = q[0]
    for c in range(1, CHIPS):
        total = total + q[c]
    columns = jnp.concatenate([total, jnp.zeros((120, 128), F32)], axis=0).T
    alpha = steps[1] * columns[:LOADS, 0:1] / (columns[:LOADS, 1:2] + 1e-6)
    multipliers[...] = mult[...] + alpha * s2[...]
    residual[...] = r1[...] - alpha * i[...]


def spread(array, axes):
    return lax.all_to_all(array, axes, 0, 0, tiled=True)


def other_core(array):
    return lax.ppermute(array, "core", [(0, 1), (1, 0)])


def shards(rhs, dual_block, schur_block, dual_scale, dof_order, modes, coarse_inverse, step_scale):
    place = pl.pallas_call(place_body, out_shape=out(10, dtype=jnp.int32), out_specs=SMEM, name="place")()
    r0 = rhs[0, 0, 0]
    dual = dual_block[0, 0, 0]
    schur = schur_block[0, 0, 0]
    scale = dual_scale[0, 0, 0]
    scale = scale.reshape(1, M)
    order = dof_order[0, 0, 0].reshape(1, M)
    modes_t = modes[0, 0, 0].T

    dealt = call(deal_body, out(LINE, 40, 128), (coarse_inverse,), 0, name="deal")
    own = spread(dealt, ("gy", "gc"))
    near = [own]
    for axis, count in (("gy", N_Y), ("gc", CHIPS)):
        for which in range(2):
            near.append(lax.ppermute(own, axis, pairs(count, which)))

    picks = call(picks_body, out(M, M, dtype=BF16), (order,), 0, name="picks")
    field = out(LOADS, M)
    faces = [out(LOADS, FACE)] * 6

    w, *sends = call(
        first_body, [field] + [out(LOADS + MODES, FACE)] * 6, (place, r0, schur, picks, modes_t), name="first"
    )
    found = swap(sends)
    m_high, m_low = call(
        modes_body,
        [out(256, M, dtype=BF16)] * 2,
        (place, modes_t, *found),
        scratch=[pltpu.VMEM((256, M), F32)],
        name="modes",
    )
    c_high, c_low = call(coarse_body, [out(5 * COLS, ROWS, dtype=BF16)] * 2, near, 0, name="coarse")

    def weigh(w, found, partial=()):
        return call(
            assemble_body, [field, out(LINE, 16, 128)], (place, w, *found, modes_t, *partial), name="assemble"
        )

    def solve(pay):
        pay = spread(pay, ("gy", "gc"))
        keep, send = call(
            coarse_product_body,
            [out(N_X, SLOTS, 128)] * 2,
            (place, pay, c_high, c_low),
            scratch=[pltpu.VMEM((5 * COLS, 128), F32)],
            name="product",
        )
        return spread(keep + other_core(send), "gx")

    def project(w, found, partial=()):
        a, pay = weigh(w, found, partial)
        return a, solve(pay)

    a, pay = weigh(w, found)
    pay, c_high, c_low, m_high, m_low = lax.optimization_barrier((pay, c_high, c_low, m_high, m_low))
    q = solve(pay)
    s, w, *sends = call(
        second_body, [field, field] + faces, (place, a, q, m_high, m_low, scale, dual, picks), name="second"
    )
    a, q = project(w, swap(sends))
    i, partial, w, *sends = call(
        third_body,
        [field, out(8, 128), field] + faces,
        (place, a, q, m_high, m_low, r0, schur, picks),
        name="third",
    )
    a, q = project(w, swap(sends), (partial,))
    mult, s2, r1, w, *sends = call(
        fourth_body,
        [field] * 4 + faces,
        (place, step_scale, a, q, m_high, m_low, r0, i, s, scale, dual, picks),
        2,
        name="fourth",
    )
    a, q = project(w, swap(sends))
    i2, pay = call(fifth_body, [field, out(PLANE, 8, 128)], (a, q, m_high, m_low, r1), 0, name="fifth")
    total = call(sum_body, out(8, 128), (spread(pay, ("gx", "gy")),), 0, name="sum")
    q = spread(call(share_body, out(CHIPS, 8, 128), (total, other_core(total)), 0, name="share"), "gc")
    multipliers, residual = call(last_body, [field] * 2, (step_scale, q, mult, s2, r1, i2), name="last")
    return (multipliers[None, None, None], residual[None, None, None])


def solution(mesh):
    mesh = Mesh(mesh.devices.reshape(N_X, N_Y, CHIPS, 2), ("gx", "gy", "gc", "core"))
    cell = lambda rest: P("gx", "gy", Z, *([None] * rest))
    in_specs = (cell(2), cell(2), cell(2), cell(1), cell(1), cell(2), P(("gx", "gy", "gc", "core"), None), P())
    return jax.shard_map(shards, mesh=mesh, in_specs=in_specs, out_specs=(cell(2), cell(2)), check_vma=False)
```

```python
import jax
import jax.numpy as jnp
from jax import lax
from jax.experimental import pallas as pl
from jax.experimental.pallas import tpu as pltpu
from jax.sharding import Mesh
from jax.sharding import PartitionSpec as P

F32 = jnp.float32
BF16 = jnp.bfloat16

LOADS = 64
MODES = 24
FACE = 256
M = 6 * FACE
N_X, N_Y, N_Z = 4, 4, 16
PLANE = N_X * N_Y
CHIPS = N_Z // 2
COLS = N_Z * MODES
ROWS = PLANE * MODES
SLOTS = 88
Z = ("gc", "core")
NT = (((1,), (1,)), ((), ()))
NN = (((1,), (0,)), ((), ()))

VMEM = pl.BlockSpec(memory_space=pltpu.VMEM)
SMEM = pl.BlockSpec(memory_space=pltpu.SMEM)


def mm(a, b, dims=NN):
    return lax.dot_general(a, b, dims, preferred_element_type=F32)


def split(value):
    high = value.astype(BF16)
    return high, (value - high.astype(F32)).astype(BF16)


def call(body, outs, args, scalars=1, scratch=(), name=None):
    return pl.pallas_call(
        body,
        out_shape=outs,
        in_specs=[SMEM] * scalars + [VMEM] * (len(args) - scalars),
        out_specs=jax.tree.map(lambda _: VMEM, outs),
        scratch_shapes=list(scratch),
        compiler_params=pltpu.CompilerParams(vmem_limit_bytes=16 * 1024 * 1024),
        name=name,
    )(*args)


def out(*dims, dtype=F32):
    return jax.ShapeDtypeStruct(dims, dtype)


def place_body(place, no, yes):
    no[0] = 0
    yes[0] = 1
    at = [lax.axis_index("gx"), lax.axis_index("gy"), 2 * lax.axis_index("gc") + lax.axis_index("core")]
    for direction, (index, end) in enumerate(zip(at, (N_X - 1, N_Y - 1, N_Z - 1))):
        place[direction] = 1 - index % 2
        place[3 + direction] = jnp.minimum(index, 1)
        place[6 + direction] = jnp.minimum(end - index, 1)


def pairs(count, which):
    forward = [(i, (i + 1) % count) for i in range(which, count, 2)]
    return forward + [(b, a) for a, b in forward]


def swap(arrays):
    found = []
    for direction, (axis, count) in enumerate((("gx", N_X), ("gy", N_Y), (Z, N_Z))):
        for which in range(2):
            found.append(lax.ppermute(arrays[2 * direction + which], axis, pairs(count, which)))
    return found


def local_product(u, block, picks):
    rows = u.shape[0]
    placed = mm(u, picks, NT).astype(BF16)
    image = mm(placed, block)
    if rows == 2 * LOADS:
        image = image[:LOADS] + image[LOADS:]
    high, low = split(image)
    back = mm(jnp.concatenate([high, low], axis=0), picks)
    return back[:LOADS] + back[LOADS:]


def send_faces(place, w, sends, extra=None):
    for direction in range(3):
        even = place[direction] == 1
        lo = 2 * direction * FACE
        for array, row in ((w, 0), (extra, LOADS)):
            if array is None:
                continue
            lower = array[:, lo : lo + FACE]
            upper = array[:, lo + FACE : lo + 2 * FACE]
            height = array.shape[0]
            sends[2 * direction][row : row + height, :] = jnp.where(even, upper, lower)
            sends[2 * direction + 1][row : row + height, :] = jnp.where(even, lower, upper)


def picks_body(order, picks):
    def fill(block, carry):
        start = pl.multiple_of(block * FACE, FACE)
        rows = lax.broadcasted_iota(jnp.int32, (FACE, M), 0) + start
        picks[pl.ds(start, FACE), :] = jnp.where(rows == order[0:1, :], 1.0, 0.0).astype(BF16)
        return carry

    lax.fori_loop(0, 6, fill, 0)


def coarse_body(*refs):
    blocks, (high, low) = refs[:5], refs[5:]
    for index, block in enumerate(blocks):
        parts = block[...].reshape(PLANE, MODES, COLS)
        ordered = [parts[:, :16].reshape(PLANE * 16, COLS), parts[:, 16:].reshape(PLANE * 8, COLS)]
        h, l = split(jnp.concatenate(ordered, axis=0).T)
        high[index * COLS : (index + 1) * COLS, :] = h
        low[index * COLS : (index + 1) * COLS, :] = l


def first_body(place, r, block, picks, modes_t, w, *sends):
    value = local_product(r[...].astype(BF16), block[...], picks[...])
    w[...] = value
    send_faces(place, value, sends, modes_t[...])


def modes_body(place, modes_t, *refs):
    found, (high, low), full = refs[:6], refs[6:8], refs[8]
    full[...] = jnp.zeros((2 * 128, M), F32)
    full[0:MODES, :] = modes_t[...]

    def put(rows, direction, source, gate_lower, gate_upper):
        lo = 2 * direction * FACE
        for row, first, last in rows:
            value = found[source][LOADS + first : LOADS + last, :]
            full[row : row + last - first, lo : lo + FACE] = jnp.where(gate_lower, value, 0.0)
            full[row : row + last - first, lo + FACE : lo + 2 * FACE] = jnp.where(gate_upper, value, 0.0)

    def gates(direction, which):
        even = place[direction] == (1 - which)
        odd = place[direction] == which
        return (
            jnp.logical_and(odd, place[3 + direction] == 1),
            jnp.logical_and(even, place[6 + direction] == 1),
        )

    for which in range(2):
        for direction in range(2):
            lower, upper = gates(direction, which)
            slot = 2 * direction + which
            rows = [(128 + slot * MODES, 0, MODES)] if slot < 3 else [(128 + 3 * MODES, 0, 16), (80, 16, MODES)]
            put(rows, direction, slot, lower, upper)
    even = place[2] == 1
    lo = 4 * FACE
    from_lower = jnp.where(even, found[5][LOADS : LOADS + MODES, :], found[4][LOADS : LOADS + MODES, :])
    from_upper = jnp.where(even, found[4][LOADS : LOADS + MODES, :], found[5][LOADS : LOADS + MODES, :])
    full[MODES : 2 * MODES, lo : lo + FACE] = jnp.where(place[5] == 1, from_lower, 0.0)
    full[2 * MODES : 3 * MODES, lo + FACE : lo + 2 * FACE] = jnp.where(place[8] == 1, from_upper, 0.0)
    h, l = split(full[...])
    high[...] = h
    low[...] = l


def assemble_body(place, w, *refs):
    found, modes_t = refs[:6], refs[6]
    partial = refs[7] if len(refs) == 10 else None
    a, pay = refs[-2:]
    for direction in range(3):
        even = place[direction] == 1
        lo = 2 * direction * FACE
        first = found[2 * direction][0:LOADS, :]
        second = found[2 * direction + 1][0:LOADS, :]
        from_lower = jnp.where(even, second, first)
        from_upper = jnp.where(even, first, second)
        a[:, lo : lo + FACE] = w[:, lo : lo + FACE] + jnp.where(place[3 + direction] == 1, from_lower, 0.0)
        a[:, lo + FACE : lo + 2 * FACE] = w[:, lo + FACE : lo + 2 * FACE] + jnp.where(
            place[6 + direction] == 1, from_upper, 0.0
        )
    a_high, a_low = split(a[...])
    m = modes_t[...]
    m_high = m.astype(BF16).astype(F32)
    stack = jnp.concatenate([m_high, m - m_high], axis=0).astype(BF16)
    both = mm(stack, jnp.concatenate([a_high, a_low], axis=0), NT)
    both = both[:MODES] + both[MODES:]
    both = both + pltpu.roll(both, LOADS, 1)
    rest = jnp.zeros((8, 128), F32) if partial is None else partial[...]
    left = lax.broadcasted_iota(jnp.int32, (16, 128), 1) < LOADS
    packed = jnp.where(left, both[:16], jnp.concatenate([both[16:], rest], axis=0))
    for p in range(PLANE):
        pay[p] = packed


def coarse_product_body(place, pay, high, low, keep, send, y):
    def half(rows, keep_left):
        value = pay[:, 0:rows, :].reshape(PLANE * rows, 128)
        left = lax.broadcasted_iota(jnp.int32, value.shape, 1) < LOADS
        return jnp.where(left == keep_left, value, pltpu.roll(value, LOADS, 1))

    x_high, x_low = split(jnp.concatenate([half(16, True), half(8, False)], axis=0))
    both = jnp.concatenate([x_high, x_low], axis=1)

    def some(block, carry):
        rows = pl.ds(pl.multiple_of(block * COLS, COLS), COLS)
        found = mm(high[rows, :], both)
        y[rows, :] = found[:, :128] + found[:, 128:] + mm(low[rows, :], x_high)
        return carry

    lax.fori_loop(0, 5, some, 0)
    rest = pay[0, 8:16, :]
    for p in range(1, PLANE):
        rest = rest + pay[p, 8:16, :]
    rest = pltpu.roll(rest, LOADS, 1)
    left = lax.broadcasted_iota(jnp.int32, (MODES, 128), 1) < LOADS
    even = place[2] == 1

    def at(block, z):
        row = block * COLS + (z % N_Z) * MODES
        return y[row : row + MODES, :]

    def chunk(z):
        last = at(4, z)
        return [
            jnp.where(left, at(0, z), at(1, z)),
            jnp.where(left, at(0, z - 1), at(2, z)),
            jnp.where(left, at(0, z + 1), at(3, z)),
            jnp.where(left[:16], jnp.concatenate([rest, last[16:]], axis=0), last[:16]),
        ]

    for c in range(CHIPS):
        for index, (zero, one) in enumerate(zip(chunk(2 * c), chunk(2 * c + 1))):
            rows = slice(index * MODES, index * MODES + zero.shape[0])
            keep[c, rows, :] = jnp.where(even, zero, one)
            send[c, rows, :] = jnp.where(even, one, zero)


def corrected(a, q, m_high, m_low):
    y = q[0]
    for c in range(1, CHIPS):
        y = y + q[c]
    y_t = jnp.concatenate([y, jnp.zeros((128 - SLOTS, 128), F32)], axis=0).T
    totals = y_t[:LOADS, 3 * MODES : 3 * MODES + 8]
    y_full = jnp.concatenate([y_t[:LOADS], y_t[LOADS:]], axis=1)
    y_high, y_low = split(y_full)
    found = mm(jnp.concatenate([y_high, y_low], axis=0), m_high[...])
    found = found[:LOADS] + found[LOADS:] + mm(y_high, m_low[...])
    return a[...] - found, totals


def products(first, second):
    lanes = lax.broadcasted_iota(jnp.int32, (LOADS, 128), 1)
    along = jnp.sum(first * second, axis=1, keepdims=True)
    energy = jnp.sum(second * second, axis=1, keepdims=True)
    both = jnp.where(lanes == 0, along, jnp.where(lanes == 1, energy, 0.0))
    return jnp.concatenate([both, both], axis=0).T[0:8, :]


def dual_body(place, steps, later, a, q, m_high, m_low, base, scale, block, picks, s, alpha, w, *sends):
    change, totals = corrected(a, q, m_high, m_low)
    rate = jnp.where(later[0] == 1, steps[0] * totals[:, 0:1] / (totals[:, 1:2] + 1e-6), -1.0)
    value = jnp.where(later[0] == 1, base[...], 0.0) - rate * change
    s[...] = value
    alpha[...] = jnp.broadcast_to(rate, (LOADS, 128))
    found = scale[...] * local_product((scale[...] * value).astype(BF16), block[...], picks[...])
    w[...] = found
    send_faces(place, found, sends)


def third_body(place, a, q, m_high, m_low, r, block, picks, unread, i, partial, w, *sends):
    value, _ = corrected(a, q, m_high, m_low)
    i[...] = value
    partial[...] = products(r[...], value)
    high, low = split(value)
    found = local_product(jnp.concatenate([high, low], axis=0), block[...], picks[...])
    w[...] = found
    send_faces(place, found, sends)


def fifth_body(a, q, m_high, m_low, r, i, alpha, i2, r1, pay):
    value, _ = corrected(a, q, m_high, m_low)
    i2[...] = value
    residual = r[...] - alpha[:, 0:1] * i[...]
    r1[...] = residual
    partial = products(residual, value)
    for p in range(PLANE):
        pay[p] = partial


def sum_body(pay, total):
    value = pay[0]
    for p in range(1, PLANE):
        value = value + pay[p]
    total[...] = value


def share_body(mine, other, copies):
    for c in range(CHIPS):
        copies[c] = mine[...] + other[...]


def last_body(steps, q, first, s, s2, r1, i, multipliers, residual):
    total = q[0]
    for c in range(1, CHIPS):
        total = total + q[c]
    columns = jnp.concatenate([total, jnp.zeros((120, 128), F32)], axis=0).T
    alpha = steps[1] * columns[:LOADS, 0:1] / (columns[:LOADS, 1:2] + 1e-6)
    multipliers[...] = first[:, 0:1] * s[...] + alpha * s2[...]
    residual[...] = r1[...] - alpha * i[...]


def spread(array, axes):
    return lax.all_to_all(array, axes, 0, 0, tiled=True)


def other_core(array):
    return lax.ppermute(array, "core", [(0, 1), (1, 0)])


def shards(rhs, dual_block, schur_block, dual_scale, dof_order, modes, coarse_inverse, step_scale):
    number = lambda n: out(n, dtype=jnp.int32)
    place, no, yes = pl.pallas_call(
        place_body, out_shape=[number(9), number(1), number(1)], out_specs=[SMEM] * 3, name="place"
    )()
    r0 = rhs[0, 0, 0]
    dual = dual_block[0, 0, 0]
    schur = schur_block[0, 0, 0]
    scale = dual_scale[0, 0, 0]
    scale = scale.reshape(1, M)
    order = dof_order[0, 0, 0].reshape(1, M)
    modes_t = modes[0, 0, 0].T

    own = spread(coarse_inverse.reshape(MODES, PLANE, COLS).transpose(1, 0, 2), ("gx", "gy")).reshape(ROWS, COLS)
    near = [own]
    for axis, count in (("gx", N_X), ("gy", N_Y)):
        for which in range(2):
            near.append(lax.ppermute(own, axis, pairs(count, which)))

    picks = call(picks_body, out(M, M, dtype=BF16), (order,), 0, name="picks")
    field = out(LOADS, M)
    faces = [out(LOADS, FACE)] * 6

    w, *sends = call(
        first_body, [field] + [out(LOADS + MODES, FACE)] * 6, (place, r0, schur, picks, modes_t), name="first"
    )
    found = swap(sends)
    m_high, m_low = call(
        modes_body,
        [out(256, M, dtype=BF16)] * 2,
        (place, modes_t, *found),
        scratch=[pltpu.VMEM((256, M), F32)],
        name="modes",
    )
    c_high, c_low = call(coarse_body, [out(5 * COLS, ROWS, dtype=BF16)] * 2, near, 0, name="coarse")

    def weigh(w, found, partial=()):
        return call(
            assemble_body, [field, out(PLANE, 16, 128)], (place, w, *found, modes_t, *partial), name="assemble"
        )

    def solve(pay):
        pay = spread(pay, ("gx", "gy"))
        keep, send = call(
            coarse_product_body,
            [out(CHIPS, SLOTS, 128)] * 2,
            (place, pay, c_high, c_low),
            scratch=[pltpu.VMEM((5 * COLS, 128), F32)],
            name="product",
        )
        return spread(keep + other_core(send), "gc")

    def project(w, found, partial=()):
        a, pay = weigh(w, found, partial)
        return a, solve(pay)

    a, pay = weigh(w, found)
    pay, c_high, c_low, m_high, m_low = lax.optimization_barrier((pay, c_high, c_low, m_high, m_low))
    q = solve(pay)
    def dual_step(later, a, q, base):
        return call(
            dual_body,
            [field, out(LOADS, 128), field] + faces,
            (place, step_scale, later, a, q, m_high, m_low, base, scale, dual, picks),
            3,
            name="dual",
        )

    s, unread, w, *sends = dual_step(no, a, q, r0)
    a, q = project(w, swap(sends))
    i, partial, w, *sends = call(
        third_body,
        [field, out(8, 128), field] + faces,
        (place, a, q, m_high, m_low, r0, schur, picks, unread),
        name="third",
    )
    a, q = project(w, swap(sends), (partial,))
    s2, alpha, w, *sends = dual_step(yes, a, q, s)
    a, q = project(w, swap(sends))
    i2, r1, pay = call(
        fifth_body, [field, field, out(PLANE, 8, 128)], (a, q, m_high, m_low, r0, i, alpha), 0, name="fifth"
    )
    total = call(sum_body, out(8, 128), (spread(pay, ("gx", "gy")),), 0, name="sum")
    q = spread(call(share_body, out(CHIPS, 8, 128), (total, other_core(total)), 0, name="share"), "gc")
    multipliers, residual = call(last_body, [field] * 2, (step_scale, q, alpha, s, s2, r1, i2), name="last")
    return (multipliers[None, None, None], residual[None, None, None])


def solution(mesh):
    mesh = Mesh(mesh.devices.reshape(N_X, N_Y, CHIPS, 2), ("gx", "gy", "gc", "core"))
    cell = lambda rest: P("gx", "gy", Z, *([None] * rest))
    in_specs = (cell(2), cell(2), cell(2), cell(1), cell(1), cell(2), P(("gx", "gy", "gc", "core"), None), P())
    return jax.shard_map(shards, mesh=mesh, in_specs=in_specs, out_specs=(cell(2), cell(2)), check_vma=False)
```

```python
import jax
import jax.numpy as jnp
from jax import lax
from jax.experimental import pallas as pl
from jax.experimental.pallas import tpu as pltpu
from jax.sharding import Mesh
from jax.sharding import PartitionSpec as P

F32 = jnp.float32
BF16 = jnp.bfloat16

LOADS = 64
MODES = 24
FACE = 256
M = 6 * FACE
N_X, N_Y, N_Z = 4, 4, 16
PLANE = N_X * N_Y
CHIPS = N_Z // 2
COLS = N_Z * MODES
ROWS = PLANE * MODES
SLOTS = 88
STEP = 5 * COLS // 2
Z = ("gc", "core")
NT = (((1,), (1,)), ((), ()))
NN = (((1,), (0,)), ((), ()))

VMEM = pl.BlockSpec(memory_space=pltpu.VMEM)
SMEM = pl.BlockSpec(memory_space=pltpu.SMEM)


def mm(a, b, dims=NN):
    return lax.dot_general(a, b, dims, preferred_element_type=F32)


def split(value):
    high = value.astype(BF16)
    return high, (value - high.astype(F32)).astype(BF16)


def call(body, outs, args, scalars=1, scratch=(), name=None):
    return pl.pallas_call(
        body,
        out_shape=outs,
        in_specs=[SMEM] * scalars + [VMEM] * (len(args) - scalars),
        out_specs=jax.tree.map(lambda _: VMEM, outs),
        scratch_shapes=list(scratch),
        compiler_params=pltpu.CompilerParams(vmem_limit_bytes=16 * 1024 * 1024),
        name=name,
    )(*args)


def out(*dims, dtype=F32):
    return jax.ShapeDtypeStruct(dims, dtype)


def place_body(place):
    at = [lax.axis_index("gx"), lax.axis_index("gy"), 2 * lax.axis_index("gc") + lax.axis_index("core")]
    for direction, (index, end) in enumerate(zip(at, (N_X - 1, N_Y - 1, N_Z - 1))):
        place[direction] = 1 - index % 2
        place[3 + direction] = jnp.minimum(index, 1)
        place[6 + direction] = jnp.minimum(end - index, 1)


def pairs(count, which):
    forward = [(i, (i + 1) % count) for i in range(which, count, 2)]
    return forward + [(b, a) for a, b in forward]


def swap(arrays):
    found = []
    for direction, (axis, count) in enumerate((("gx", N_X), ("gy", N_Y), (Z, N_Z))):
        for which in range(2):
            found.append(lax.ppermute(arrays[2 * direction + which], axis, pairs(count, which)))
    return found


def local_product(u, block, picks):
    rows = u.shape[0]
    placed = mm(u, picks, NT).astype(BF16)
    image = mm(placed, block)
    if rows == 2 * LOADS:
        image = image[:LOADS] + image[LOADS:]
    high, low = split(image)
    back = mm(jnp.concatenate([high, low], axis=0), picks)
    return back[:LOADS] + back[LOADS:]


def send_faces(place, w, sends, extra=None):
    for direction in range(3):
        even = place[direction] == 1
        lo = 2 * direction * FACE
        for array, row in ((w, 0), (extra, LOADS)):
            if array is None:
                continue
            lower = array[:, lo : lo + FACE]
            upper = array[:, lo + FACE : lo + 2 * FACE]
            height = array.shape[0]
            sends[2 * direction][row : row + height, :] = jnp.where(even, upper, lower)
            sends[2 * direction + 1][row : row + height, :] = jnp.where(even, lower, upper)


def picks_body(order, picks):
    def fill(block, carry):
        start = pl.multiple_of(block * FACE, FACE)
        rows = lax.broadcasted_iota(jnp.int32, (FACE, M), 0) + start
        picks[pl.ds(start, FACE), :] = jnp.where(rows == order[0:1, :], 1.0, 0.0).astype(BF16)
        return carry

    lax.fori_loop(0, 6, fill, 0)


def coarse_body(*refs):
    blocks, (high, low) = refs[:5], refs[5:]
    for index, block in enumerate(blocks):
        parts = block[...].reshape(PLANE, MODES, COLS)
        ordered = [parts[:, :16].reshape(PLANE * 16, COLS), parts[:, 16:].reshape(PLANE * 8, COLS)]
        h, l = split(jnp.concatenate(ordered, axis=0).T)
        high[index * COLS : (index + 1) * COLS, :] = h
        low[index * COLS : (index + 1) * COLS, :] = l


def first_body(place, r, block, picks, modes_t, w, *sends):
    value = local_product(r[...].astype(BF16), block[...], picks[...])
    w[...] = value
    send_faces(place, value, sends, modes_t[...])


def modes_body(place, modes_t, *refs):
    found, (high, low), full = refs[:6], refs[6:8], refs[8]
    full[...] = jnp.zeros((2 * 128, M), F32)
    full[0:MODES, :] = modes_t[...]

    def put(rows, direction, source, gate_lower, gate_upper):
        lo = 2 * direction * FACE
        for row, first, last in rows:
            value = found[source][LOADS + first : LOADS + last, :]
            full[row : row + last - first, lo : lo + FACE] = jnp.where(gate_lower, value, 0.0)
            full[row : row + last - first, lo + FACE : lo + 2 * FACE] = jnp.where(gate_upper, value, 0.0)

    def gates(direction, which):
        even = place[direction] == (1 - which)
        odd = place[direction] == which
        return (
            jnp.logical_and(odd, place[3 + direction] == 1),
            jnp.logical_and(even, place[6 + direction] == 1),
        )

    for which in range(2):
        for direction in range(2):
            lower, upper = gates(direction, which)
            slot = 2 * direction + which
            rows = [(128 + slot * MODES, 0, MODES)] if slot < 3 else [(128 + 3 * MODES, 0, 16), (80, 16, MODES)]
            put(rows, direction, slot, lower, upper)
    even = place[2] == 1
    lo = 4 * FACE
    from_lower = jnp.where(even, found[5][LOADS : LOADS + MODES, :], found[4][LOADS : LOADS + MODES, :])
    from_upper = jnp.where(even, found[4][LOADS : LOADS + MODES, :], found[5][LOADS : LOADS + MODES, :])
    full[MODES : 2 * MODES, lo : lo + FACE] = jnp.where(place[5] == 1, from_lower, 0.0)
    full[2 * MODES : 3 * MODES, lo + FACE : lo + 2 * FACE] = jnp.where(place[8] == 1, from_upper, 0.0)
    h, l = split(full[...])
    high[...] = h
    low[...] = l


def assemble_body(place, w, *refs):
    found, modes_t = refs[:6], refs[6]
    partial = refs[7] if len(refs) == 10 else None
    a, pay = refs[-2:]
    for direction in range(3):
        even = place[direction] == 1
        lo = 2 * direction * FACE
        first = found[2 * direction][0:LOADS, :]
        second = found[2 * direction + 1][0:LOADS, :]
        from_lower = jnp.where(even, second, first)
        from_upper = jnp.where(even, first, second)
        a[:, lo : lo + FACE] = w[:, lo : lo + FACE] + jnp.where(place[3 + direction] == 1, from_lower, 0.0)
        a[:, lo + FACE : lo + 2 * FACE] = w[:, lo + FACE : lo + 2 * FACE] + jnp.where(
            place[6 + direction] == 1, from_upper, 0.0
        )
    a_high, a_low = split(a[...])
    m = modes_t[...]
    m_high = m.astype(BF16).astype(F32)
    stack = jnp.concatenate([m_high, m - m_high], axis=0).astype(BF16)
    both = mm(stack, jnp.concatenate([a_high, a_low], axis=0), NT)
    both = both[:MODES] + both[MODES:]
    both = both + pltpu.roll(both, LOADS, 1)
    rest = jnp.zeros((8, 128), F32) if partial is None else partial[...]
    left = lax.broadcasted_iota(jnp.int32, (16, 128), 1) < LOADS
    packed = jnp.where(left, both[:16], jnp.concatenate([both[16:], rest], axis=0))
    for p in range(PLANE):
        pay[p] = packed


def coarse_product_body(place, pay, high, low, keep, send, y):
    def half(rows, keep_left):
        value = pay[:, 0:rows, :].reshape(PLANE * rows, 128)
        left = lax.broadcasted_iota(jnp.int32, value.shape, 1) < LOADS
        return jnp.where(left == keep_left, value, pltpu.roll(value, LOADS, 1))

    x_high, x_low = split(jnp.concatenate([half(16, True), half(8, False)], axis=0))
    both = jnp.concatenate([x_high, x_low], axis=1)

    def some(part, carry):
        rows = pl.ds(pl.multiple_of(part * STEP, STEP), STEP)
        found = mm(high[rows, :], both)
        y[rows, :] = found[:, :128] + found[:, 128:] + mm(low[rows, :], x_high)
        return carry

    lax.fori_loop(0, 2, some, 0)
    rest = pay[0, 8:16, :]
    for p in range(1, PLANE):
        rest = rest + pay[p, 8:16, :]
    rest = pltpu.roll(rest, LOADS, 1)
    left = lax.broadcasted_iota(jnp.int32, (MODES, 128), 1) < LOADS
    even = place[2] == 1

    def at(block, z):
        row = block * COLS + (z % N_Z) * MODES
        return y[row : row + MODES, :]

    def chunk(z):
        last = at(4, z)
        return [
            jnp.where(left, at(0, z), at(1, z)),
            jnp.where(left, at(0, z - 1), at(2, z)),
            jnp.where(left, at(0, z + 1), at(3, z)),
            jnp.where(left[:16], jnp.concatenate([rest, last[16:]], axis=0), last[:16]),
        ]

    for c in range(CHIPS):
        for index, (zero, one) in enumerate(zip(chunk(2 * c), chunk(2 * c + 1))):
            rows = slice(index * MODES, index * MODES + zero.shape[0])
            keep[c, rows, :] = jnp.where(even, zero, one)
            send[c, rows, :] = jnp.where(even, one, zero)


def corrected(a, q, m_high, m_low):
    y = q[0]
    for c in range(1, CHIPS):
        y = y + q[c]
    y_t = jnp.concatenate([y, jnp.zeros((128 - SLOTS, 128), F32)], axis=0).T
    totals = y_t[:LOADS, 3 * MODES : 3 * MODES + 8]
    y_full = jnp.concatenate([y_t[:LOADS], y_t[LOADS:]], axis=1)
    y_high, y_low = split(y_full)
    found = mm(jnp.concatenate([y_high, y_low], axis=0), m_high[...])
    found = found[:LOADS] + found[LOADS:] + mm(y_high, m_low[...])
    return a[...] - found, totals


def products(first, second):
    lanes = lax.broadcasted_iota(jnp.int32, (LOADS, 128), 1)
    along = jnp.sum(first * second, axis=1, keepdims=True)
    energy = jnp.sum(second * second, axis=1, keepdims=True)
    both = jnp.where(lanes == 0, along, jnp.where(lanes == 1, energy, 0.0))
    return jnp.concatenate([both, both], axis=0).T[0:8, :]


def second_body(place, a, q, m_high, m_low, scale, block, picks, s, w, *sends):
    value, _ = corrected(a, q, m_high, m_low)
    s[...] = value
    found = scale[...] * local_product((scale[...] * value).astype(BF16), block[...], picks[...])
    w[...] = found
    send_faces(place, found, sends)


def third_body(place, a, q, m_high, m_low, r, block, picks, i, partial, w, *sends):
    value, _ = corrected(a, q, m_high, m_low)
    i[...] = value
    partial[...] = products(r[...], value)
    high, low = split(value)
    found = local_product(jnp.concatenate([high, low], axis=0), block[...], picks[...])
    w[...] = found
    send_faces(place, found, sends)


def fourth_body(place, steps, a, q, m_high, m_low, r, i, s, scale, block, picks, mult, s2, r1, w, *sends):
    t, totals = corrected(a, q, m_high, m_low)
    alpha = steps[0] * totals[:, 0:1] / (totals[:, 1:2] + 1e-6)
    value = s[...] - alpha * t
    s2[...] = value
    mult[...] = alpha * s[...]
    r1[...] = r[...] - alpha * i[...]
    found = scale[...] * local_product((scale[...] * value).astype(BF16), block[...], picks[...])
    w[...] = found
    send_faces(place, found, sends)


def fifth_body(a, q, m_high, m_low, r1, i, pay):
    value, _ = corrected(a, q, m_high, m_low)
    i[...] = value
    partial = products(r1[...], value)
    for p in range(PLANE):
        pay[p] = partial


def sum_body(pay, total):
    value = pay[0]
    for p in range(1, PLANE):
        value = value + pay[p]
    total[...] = value


def share_body(mine, other, copies):
    for c in range(CHIPS):
        copies[c] = mine[...] + other[...]


def last_body(steps, q, mult, s2, r1, i, multipliers, residual):
    total = q[0]
    for c in range(1, CHIPS):
        total = total + q[c]
    columns = jnp.concatenate([total, jnp.zeros((120, 128), F32)], axis=0).T
    alpha = steps[1] * columns[:LOADS, 0:1] / (columns[:LOADS, 1:2] + 1e-6)
    multipliers[...] = mult[...] + alpha * s2[...]
    residual[...] = r1[...] - alpha * i[...]


def spread(array, axes):
    return lax.all_to_all(array, axes, 0, 0, tiled=True)


def other_core(array):
    return lax.ppermute(array, "core", [(0, 1), (1, 0)])


def shards(rhs, dual_block, schur_block, dual_scale, dof_order, modes, coarse_inverse, step_scale):
    place = pl.pallas_call(place_body, out_shape=out(9, dtype=jnp.int32), out_specs=SMEM, name="place")()
    r0 = rhs[0, 0, 0]
    dual = dual_block[0, 0, 0]
    schur = schur_block[0, 0, 0]
    scale = dual_scale[0, 0, 0]
    scale = scale.reshape(1, M)
    order = dof_order[0, 0, 0].reshape(1, M)
    modes_t = modes[0, 0, 0].T

    own = spread(coarse_inverse.reshape(MODES, PLANE, COLS).transpose(1, 0, 2), ("gx", "gy")).reshape(ROWS, COLS)
    near = [own]
    for axis, count in (("gx", N_X), ("gy", N_Y)):
        for which in range(2):
            near.append(lax.ppermute(own, axis, pairs(count, which)))

    picks = call(picks_body, out(M, M, dtype=BF16), (order,), 0, name="picks")
    field = out(LOADS, M)
    faces = [out(LOADS, FACE)] * 6

    w, *sends = call(
        first_body, [field] + [out(LOADS + MODES, FACE)] * 6, (place, r0, schur, picks, modes_t), name="first"
    )
    found = swap(sends)
    m_high, m_low = call(
        modes_body,
        [out(256, M, dtype=BF16)] * 2,
        (place, modes_t, *found),
        scratch=[pltpu.VMEM((256, M), F32)],
        name="modes",
    )
    c_high, c_low = call(coarse_body, [out(5 * COLS, ROWS, dtype=BF16)] * 2, near, 0, name="coarse")

    def weigh(w, found, partial=()):
        return call(
            assemble_body, [field, out(PLANE, 16, 128)], (place, w, *found, modes_t, *partial), name="assemble"
        )

    def solve(pay):
        pay = spread(pay, ("gx", "gy"))
        keep, send = call(
            coarse_product_body,
            [out(CHIPS, SLOTS, 128)] * 2,
            (place, pay, c_high, c_low),
            scratch=[pltpu.VMEM((5 * COLS, 128), F32)],
            name="product",
        )
        return spread(keep + other_core(send), "gc")

    def project(w, found, partial=()):
        a, pay = weigh(w, found, partial)
        return a, solve(pay)

    a, pay = weigh(w, found)
    pay, c_high, c_low, m_high, m_low = lax.optimization_barrier((pay, c_high, c_low, m_high, m_low))
    q = solve(pay)
    s, w, *sends = call(
        second_body, [field, field] + faces, (place, a, q, m_high, m_low, scale, dual, picks), name="second"
    )
    a, q = project(w, swap(sends))
    i, partial, w, *sends = call(
        third_body,
        [field, out(8, 128), field] + faces,
        (place, a, q, m_high, m_low, r0, schur, picks),
        name="third",
    )
    a, q = project(w, swap(sends), (partial,))
    mult, s2, r1, w, *sends = call(
        fourth_body,
        [field] * 4 + faces,
        (place, step_scale, a, q, m_high, m_low, r0, i, s, scale, dual, picks),
        2,
        name="fourth",
    )
    a, q = project(w, swap(sends))
    i2, pay = call(fifth_body, [field, out(PLANE, 8, 128)], (a, q, m_high, m_low, r1), 0, name="fifth")
    total = call(sum_body, out(8, 128), (spread(pay, ("gx", "gy")),), 0, name="sum")
    q = spread(call(share_body, out(CHIPS, 8, 128), (total, other_core(total)), 0, name="share"), "gc")
    multipliers, residual = call(last_body, [field] * 2, (step_scale, q, mult, s2, r1, i2), name="last")
    return (multipliers[None, None, None], residual[None, None, None])


def solution(mesh):
    mesh = Mesh(mesh.devices.reshape(N_X, N_Y, CHIPS, 2), ("gx", "gy", "gc", "core"))
    cell = lambda rest: P("gx", "gy", Z, *([None] * rest))
    in_specs = (cell(2), cell(2), cell(2), cell(1), cell(1), cell(2), P(("gx", "gy", "gc", "core"), None), P())
    return jax.shard_map(shards, mesh=mesh, in_specs=in_specs, out_specs=(cell(2), cell(2)), check_vma=False)
```
